32 devices in a mesh: role: 2 (over core), seq: 4 (over z), tp: 4 (over y, x).
Axes of the slice: x: 2, y: 2, z: 4, core: 2. Of those that a mesh axis runs over, the one named last changes fastest.
Arguments:
- merger_hidden: bfloat16 [512, 5120], P(('role', 'seq'), 'tp'), may hold values from -6 to 6
- merger_out: bfloat16 [5120, 8192], P('tp', ('role', 'seq')), may hold values from -0.078125 to 0.078125
- row_position: int32 [512], P(('role', 'seq')), may hold values from -1 to 2047, as said below
- prompt_embeds: bfloat16 [2048, 8192], P(('role', 'seq'), 'tp'), may hold values from -300 to 300
- norm_gain: bfloat16 [8192], P('tp'), may hold values from 0.099609375 to 1.8984375
- query_weight: bfloat16 [8192, 4096], P(None, 'tp'), may hold values from -2.762136 to 2.762136
- key_weight: bfloat16 [8192, 512], P(None, 'tp'), may hold values from -0.06629126 to 0.06629126
- value_weight: bfloat16 [8192, 512], P(None, 'tp'), may hold values from -0.0625 to 0.0625
Outputs:
- stream: bfloat16 [2048, 8192], P(('role', 'seq'), 'tp')
- context: bfloat16 [2048, 4096], P(('role', 'seq'), 'tp')
The draws below stay inside these ranges and needn't reach their ends.
Inputs may be any that keep to these rules, and one draw needn't show every extreme that they name: `row_position`: the live slots of each device's 64 come first and hold distinct prompt positions, distinct over all devices; the other slots hold -1. Of one device's slots at most 16 hold positions of one owner's block (positions j * 256 to (j + 1) * 256 - 1); every device has 16 or more live slots.
All inputs are finite; a program needn't handle non-finite values.
Results may differ from the reference program's by a relative error of at most 0.012.
The reference program's roundings to bfloat16 on the way (of `embeds`, `normed` and `rounded`) count: a program that leaves them out, or rounds other values in their place, can miss the bound.
Values may be sent and summed in bfloat16 or wider, within the bound.
No kernel may reach another device: no remote copies, remote signals or barrier semaphores. Data moves between devices by JAX's collectives and lax.ppermute only.
A program may use at most 192 MiB of HBM per device.

```python
import math
import jax
import jax.numpy as jnp
from jax import lax

D = 8192
MH = 5120
HEAD_DIM = 128
HEADS = 32
KV_HEADS = 4
TOK_DEV = 256
ROW_DEV = 64
TOKENS = 2048
ROWS = 512
CAP = 16


def draw_row_position(key, part):
    groups = ROWS // ROW_DEV
    capacity = CAP
    items = groups * capacity
    base_key = jax.random.fold_in(key, 11)
    subkeys = jax.random.split(base_key, 4)
    shared_owner = jax.random.randint(subkeys[0], (), 0, groups)
    full_device = jax.random.randint(subkeys[1], (), 0, groups)
    exponent = jax.random.randint(subkeys[2], (groups,), 0, 4)
    divisor = jnp.array([1, 2, 4, 8], jnp.int32)[exponent]
    live_count = jnp.maximum(capacity, ROW_DEV // divisor)
    live_count = jnp.where(jnp.arange(groups) == full_device, ROW_DEV, live_count)
    device_keys = jax.random.split(subkeys[3], groups)

    def one_device(device_key, device, count):
        pick_key, order_key = jax.random.split(device_key)
        entries = jnp.arange(items, dtype=jnp.int32)
        owners = entries // capacity
        offsets = entries % capacity
        ranking = jax.random.randint(pick_key, (items,), 0, 1 << 20) * items + entries
        ranking = jnp.where(owners == shared_owner, entries - items, ranking)
        chosen = jnp.argsort(ranking)[:ROW_DEV]
        spots = owners[chosen] * TOK_DEV + device * capacity + offsets[chosen]
        slots_all = jnp.arange(ROW_DEV, dtype=jnp.int32)
        shuffle = jax.random.randint(order_key, (ROW_DEV,), 0, 1 << 20) * ROW_DEV + slots_all
        shuffle = jnp.where(slots_all < count, shuffle, (1 << 30) + slots_all)
        spots = spots[jnp.argsort(shuffle)]
        return jnp.where(slots_all < count, spots, -1)
    result = jax.vmap(one_device)(device_keys, jnp.arange(groups, dtype=jnp.int32), live_count)
    return result.reshape(ROWS).astype(jnp.int32)


def draw_prompt_embeds(key, part):
    subkeys = jax.random.split(jax.random.fold_in(key, 23), 3)
    lift = jnp.arange(D, dtype=jnp.float32) / D
    column = 0.3 * jnp.exp(jnp.log(10.0) * lift) * jnp.exp(jax.random.uniform(subkeys[0], (D,), minval=-0.2, maxval=0.2))
    row_scale = jnp.exp(jax.random.uniform(subkeys[1], (TOKENS, 1), minval=0.0, maxval=jnp.log(10.0)))
    values = jnp.clip(jax.random.normal(subkeys[2], (TOKENS, D)), -6.0, 6.0) * column[None, :] * row_scale
    return values.astype(jnp.bfloat16)


def key_table(key):
    noise = jnp.clip(jax.random.normal(jax.random.fold_in(key, 41), (D, KV_HEADS * HEAD_DIM)), -6.0, 6.0)
    return noise * D ** (-0.5)


def draw_key_weight(key, part):
    return key_table(key).astype(jnp.bfloat16)


def draw_query_weight(key, part):
    noise = jnp.clip(jax.random.normal(jax.random.fold_in(key, 43), (D, HEADS * HEAD_DIM)), -6.0, 6.0) * D ** (-0.5)
    values = 3.0 * noise
    return values.astype(jnp.bfloat16)


def level_of(stream_key, shape, cuts, smallest, top_value):
    gain, own = 1.0, jax.random.fold_in(stream_key, 6)
    for dim, shards_of in cuts:
        draws = jnp.exp(jax.random.uniform(jax.random.fold_in(own, dim), (shards_of,), jnp.float32, smallest / len(cuts), top_value / len(cuts)))
        gain = gain * jnp.repeat(draws, shape[dim] // shards_of).reshape([-1 if axis == dim else 1 for axis in range(len(shape))])
    return gain


def centred(rng, extent, width, bound, cuts=(), kind=jnp.bfloat16):
    values = jax.random.normal(rng, extent, jnp.float32) * width
    if len(cuts) > 0:
        values = level_of(rng, extent, cuts, -0.22, 0.18) * values
    return jnp.clip(values, min=-bound, max=bound).astype(kind)


def setup_inputs(seed: int = 0) -> dict:
    key_of = jax.random.split(jax.random.key(seed), 9)
    merger_hidden = centred(key_of[0], (ROWS, MH), 1.0, 6.0, ((0, 8), (1, 4)))
    merger_out = centred(key_of[1], (MH, D), MH ** -0.5, 0.078125, ((0, 4), (1, 8)))
    row_position = draw_row_position(jax.random.fold_in(key_of[8], 71), 0)
    prompt_embeds = draw_prompt_embeds(jax.random.fold_in(key_of[8], 71), 0)
    norm_gain = jnp.clip(1.0 + 0.18 * jax.random.normal(key_of[4], (D,), jnp.float32), 0.099609375, 1.8984375).astype(jnp.bfloat16)
    query_weight = draw_query_weight(jax.random.fold_in(key_of[8], 71), 0)
    key_weight = draw_key_weight(jax.random.fold_in(key_of[8], 71), 0)
    value_weight = centred(key_of[7], (D, KV_HEADS * HEAD_DIM), D ** -0.5, 0.0625, ((1, 4),))
    return {"merger_hidden": merger_hidden, "merger_out": merger_out, "row_position": row_position, "prompt_embeds": prompt_embeds, "norm_gain": norm_gain, "query_weight": query_weight, "key_weight": key_weight, "value_weight": value_weight}


def rotate(vectors, positions):
    half_dim = vectors.shape[-1] // 2
    frequency = 1000000.0 ** (-jnp.arange(half_dim, dtype=jnp.float32) / half_dim)
    angles = positions.astype(jnp.float32)[:, None, None] * frequency[None, None, :]
    cosine = jnp.cos(angles)
    sine_part = jnp.sin(angles)
    lower_half = vectors[..., :half_dim]
    upper_half = vectors[..., half_dim:]
    return jnp.concatenate([lower_half * cosine - upper_half * sine_part, upper_half * cosine + lower_half * sine_part], axis=-1)

def reference(merger_hidden, merger_out, row_position, prompt_embeds, norm_gain, query_weight, key_weight, value_weight):
    embeds = jnp.dot(merger_hidden, merger_out, preferred_element_type=jnp.float32).astype(jnp.bfloat16)
    target = jnp.where(row_position >= 0, row_position, TOKENS).astype(jnp.int32)
    stream = prompt_embeds.at[target].set(embeds, mode='drop')
    widened = stream.astype(jnp.float32)
    inverse = lax.rsqrt(lax.optimization_barrier(jnp.sum(widened * widened, axis=1, keepdims=True)) / D + 1e-06)
    normed = (widened * inverse * norm_gain.astype(jnp.float32)[None, :]).astype(jnp.bfloat16)
    positions = jnp.arange(TOKENS, dtype=jnp.int32)
    query_sum = jnp.dot(normed, query_weight, preferred_element_type=jnp.float32)
    key_sum = jnp.dot(normed, key_weight, preferred_element_type=jnp.float32)
    value_sum = jnp.dot(normed, value_weight, preferred_element_type=jnp.float32)
    queries = rotate(query_sum.reshape(TOKENS, HEADS, HEAD_DIM), positions).astype(jnp.bfloat16)
    key_rows = rotate(key_sum.reshape(TOKENS, KV_HEADS, HEAD_DIM), positions).astype(jnp.bfloat16)
    value_rows = value_sum.astype(jnp.bfloat16).reshape(TOKENS, KV_HEADS, HEAD_DIM)
    group_size = HEADS // KV_HEADS
    block = math.gcd(TOKENS, 512)
    block_count = TOKENS // block
    score_scale = 1.0 / math.sqrt(HEAD_DIM)
    every_key = jnp.arange(TOKENS, dtype=jnp.int32)

    def one_block(block_id):
        kv_head = (block_id // block_count).astype(jnp.int32)
        first_row = (block_id % block_count * block).astype(jnp.int32)
        zero_index = jnp.zeros((), jnp.int32)
        query_block = lax.dynamic_slice(queries, (first_row, kv_head * group_size, zero_index), (block, group_size, HEAD_DIM)).astype(jnp.float32)
        key_block = lax.dynamic_slice(key_rows, (zero_index, kv_head, zero_index), (TOKENS, 1, HEAD_DIM))[:, 0].astype(jnp.float32)
        value_block = lax.dynamic_slice(value_rows, (zero_index, kv_head, zero_index), (TOKENS, 1, HEAD_DIM))[:, 0].astype(jnp.float32)
        scores = jnp.einsum('qgd,kd->gqk', query_block, key_block) * score_scale
        query_pos = first_row + jnp.arange(block, dtype=jnp.int32)
        visible = every_key[None, :] <= query_pos[:, None]
        scores = jnp.where(visible[None], scores, -jnp.inf)
        row_max = lax.optimization_barrier(jnp.max(scores, axis=2, keepdims=True))
        probability = jnp.exp(scores - row_max)
        row_sum = lax.optimization_barrier(jnp.sum(probability, axis=2))
        rounded = lax.optimization_barrier(probability.astype(jnp.bfloat16))
        mixed = jnp.einsum('gqk,kd->qgd', rounded.astype(jnp.float32), value_block)
        return (mixed / jnp.transpose(row_sum)[:, :, None]).astype(jnp.bfloat16)
    blocks = lax.map(one_block, jnp.arange(KV_HEADS * block_count, dtype=jnp.int32))
    context = blocks.reshape(KV_HEADS, block_count, block, group_size, HEAD_DIM)
    context = jnp.transpose(context, (1, 2, 0, 3, 4)).reshape(TOKENS, HEADS * HEAD_DIM)
    return (stream, context)
```

```python
import functools
import math

import jax
import jax.numpy as jnp
from jax import lax
from jax.experimental import pallas as pl
from jax.experimental.pallas import tpu as pltpu
from jax.sharding import PartitionSpec as P

HEAD_DIM = 128
BF16 = jnp.bfloat16
F32 = jnp.float32


def swap(x, axis, k, keep=None):
    n = lax.axis_size(axis)
    pairs = [(i, i ^ k) for i in range(n) if keep is None or keep(i, i ^ k)]
    return lax.ppermute(x, axis, pairs)


def gather_xor(x, axis):
    return [x] + [swap(x, axis, k) for k in range(1, lax.axis_size(axis))]


def dot(a, b):
    return jnp.dot(a, b, preferred_element_type=F32)


def qkv_kernel(
    tp,
    groups,
    info,
    early_own,
    early_in,
    late_own,
    late_in,
    gain,
    cosine,
    sine,
    wq,
    wk,
    wv,
    q_out,
    kv_out,
    late_out,
    rows,
    inverse,
    acc,
):
    step = pl.program_id(0)
    me = info[0]
    early, columns = early_own.shape
    late = late_own.shape[0]
    width = rows.shape[1]
    strip = width // groups
    part = columns // groups
    q_cols, k_cols = wq.shape[1], wk.shape[1]
    v_cols = wv.shape[1]

    @pl.when(step == 0)
    def _():
        image_rows = lax.broadcasted_iota(jnp.int32, (late, 1), 0) < info[1]
        for k in range(tp):
            source = me ^ k
            base = pl.multiple_of(source * columns, columns)
            early_piece = early_own[...] if k == 0 else early_in[k - 1]
            rows[0:early, pl.ds(base, columns)] = early_piece
            late_piece = late_own[...] if k == 0 else late_in[k - 1]
            rows[early:, pl.ds(base, columns)] = late_piece
        for k in range(tp if part % 128 == 0 else 0):
            source = me ^ k
            for m in range(groups):
                at = pl.multiple_of(info[2 + m] * strip + source * part, part)
                if k == 0:
                    piece = late_own[:, m * part : (m + 1) * part]
                else:
                    piece = late_in[k - 1, :, m * part : (m + 1) * part]
                rows[early:, pl.ds(at, part)] = jnp.where(
                    image_rows, piece, rows[early:, pl.ds(at, part)]
                )
        late_out[...] = rows[early:, pl.ds(pl.multiple_of(me * columns, columns), columns)]
        total = jnp.zeros((early + late, 1), F32)
        for j in range(groups):
            piece = rows[:, j * strip : (j + 1) * strip].astype(F32)
            total = total + jnp.sum(piece * piece, axis=1, keepdims=True)
        inverse[...] = lax.rsqrt(total / width + 1e-06)
        acc[...] = jnp.zeros_like(acc)

    chunk = wq.shape[0]
    at = pl.multiple_of(step * chunk, chunk)
    scaled = rows[:, pl.ds(at, chunk)].astype(F32) * inverse[...]
    source = (step * chunk) // columns
    inner = pl.multiple_of(step * chunk - source * columns, chunk)
    weight = gain[me ^ source, :, pl.ds(inner, chunk)]
    normed = (scaled * weight).astype(BF16)
    acc[:, 0:q_cols] += dot(normed, wq[...])
    acc[:, q_cols : q_cols + k_cols] += dot(normed, wk[...])
    acc[:, q_cols + k_cols :] += dot(normed, wv[...])

    @pl.when(step == pl.num_programs(0) - 1)
    def _():
        half = HEAD_DIM // 2
        for head in range((q_cols + k_cols) // HEAD_DIM):
            first = head * HEAD_DIM
            vector = acc[:, first : first + HEAD_DIM]
            turned = jnp.concatenate([vector[:, half:], vector[:, :half]], axis=1)
            result = (vector * cosine[...] + turned * sine[...]).astype(BF16)
            if first < q_cols:
                q_out[:, first : first + HEAD_DIM] = result
            else:
                kv_out[:, first - q_cols : first - q_cols + HEAD_DIM] = result
        kv_out[:, k_cols : k_cols + v_cols] = acc[:, q_cols + k_cols :].astype(BF16)


def project(info, early_own, early_in, late_own, late_in, gain, cosine, sine, wq, wk, wv, groups):
    tp = early_in.shape[0] + 1
    early, columns = early_own.shape
    late = late_own.shape[0]
    tokens = early + late
    width = wq.shape[0]
    chunk = width // 8
    total = wq.shape[1] + wk.shape[1] + wv.shape[1]
    whole = lambda shape: pl.BlockSpec(shape, lambda j, info: (0,) * len(shape))
    return pl.pallas_call(
        functools.partial(qkv_kernel, tp, groups),
        grid_spec=pltpu.PrefetchScalarGridSpec(
            num_scalar_prefetch=1,
            grid=(width // chunk,),
            in_specs=[
                whole(early_own.shape),
                whole(early_in.shape),
                whole(late_own.shape),
                whole(late_in.shape),
                whole(gain.shape),
                whole(cosine.shape),
                whole(sine.shape),
                pl.BlockSpec((chunk, wq.shape[1]), lambda j, info: (j, 0)),
                pl.BlockSpec((chunk, wk.shape[1]), lambda j, info: (j, 0)),
                pl.BlockSpec((chunk, wv.shape[1]), lambda j, info: (j, 0)),
            ],
            out_specs=[
                whole((tokens, wq.shape[1])),
                whole((tokens, wk.shape[1] + wv.shape[1])),
                whole((late, columns)),
            ],
            scratch_shapes=[
                pltpu.VMEM((tokens, width), BF16),
                pltpu.VMEM((tokens, 1), F32),
                pltpu.VMEM((tokens, total), F32),
            ],
        ),
        out_shape=[
            jax.ShapeDtypeStruct((tokens, wq.shape[1]), BF16),
            jax.ShapeDtypeStruct((tokens, wk.shape[1] + wv.shape[1]), BF16),
            jax.ShapeDtypeStruct((late, columns), BF16),
        ],
        compiler_params=pltpu.CompilerParams(vmem_limit_bytes=48 << 20),
    )(info, early_own, early_in, late_own, late_in, gain, cosine, sine, wq, wk, wv)


def attention_kernel(pieces, group_size, blocks, q, *refs):
    kv_refs = refs[:pieces]
    q_pos, k_pos, place, out, scores = refs[pieces:]
    tokens = q.shape[0]
    scale = 1.0 / math.sqrt(HEAD_DIM)
    rank = blocks[0]
    top = None
    for j in range(pieces):
        keys = kv_refs[j][:, 0:HEAD_DIM]
        piece = lax.dot_general(
            q[...], keys, (((1,), (1,)), ((), ())), preferred_element_type=F32
        )
        piece = piece * scale
        if j == 0:
            piece = jnp.where(k_pos[...] <= q_pos[...], piece, -jnp.inf)
        else:
            piece = jnp.where(blocks[j] < rank, piece, -jnp.inf)
        scores[:, j * tokens : (j + 1) * tokens] = piece
        here = jnp.max(piece, axis=1, keepdims=True)
        top = here if top is None else jnp.maximum(top, here)
    total = None
    mixed = None
    for j in range(pieces):
        weight = jnp.exp(scores[:, j * tokens : (j + 1) * tokens] - top)
        here = jnp.sum(weight, axis=1, keepdims=True)
        total = here if total is None else total + here
        part = dot(weight.astype(BF16), kv_refs[j][:, HEAD_DIM:])
        mixed = part if mixed is None else mixed + part
    result = (mixed / total).astype(BF16)
    out[...] = dot(place[...], result).astype(BF16)


def attend(blocks, q, kvs, q_pos, k_pos, place, local_kv):
    tokens = q.shape[0]
    heads = q.shape[1] // HEAD_DIM
    group_size = heads // local_kv
    kv_spec = pl.BlockSpec((tokens, 2 * HEAD_DIM), lambda h, b: (0, h // group_size))
    whole = lambda shape: pl.BlockSpec(shape, lambda h, b: (0,) * len(shape))
    return pl.pallas_call(
        functools.partial(attention_kernel, len(kvs), group_size),
        grid_spec=pltpu.PrefetchScalarGridSpec(
            num_scalar_prefetch=1,
            grid=(heads,),
            in_specs=[pl.BlockSpec((tokens, HEAD_DIM), lambda h, b: (0, h))]
            + [kv_spec] * len(kvs)
            + [whole(q_pos.shape), whole(k_pos.shape), whole(place.shape)],
            out_specs=pl.BlockSpec((tokens, HEAD_DIM), lambda h, b: (0, h)),
            scratch_shapes=[pltpu.VMEM((tokens, tokens * len(kvs)), F32)],
        ),
        out_shape=jax.ShapeDtypeStruct(q.shape, BF16),
        compiler_params=pltpu.CompilerParams(vmem_limit_bytes=32 << 20),
    )(blocks, q, *kvs, q_pos, k_pos, place)


def natural_pieces(pieces, part, image_count):
    roles, seqs, tps = lax.axis_size("role"), lax.axis_size("seq"), lax.axis_size("tp")
    role, seq, tp = lax.axis_index("role"), lax.axis_index("seq"), lax.axis_index("tp")
    late, columns = pieces[0].shape
    by_source = jnp.stack(pieces)[jnp.arange(tps) ^ tp]
    text = jnp.transpose(by_source, (1, 0, 2))
    device = jnp.arange(roles * seqs)
    entry = ((device // seqs) ^ role) * seqs + ((device % seqs) ^ seq)
    image = by_source.reshape(tps, late, roles * seqs, part)[:, :, entry]
    image = jnp.transpose(image, (1, 2, 0, 3)).reshape(late, tps, columns)
    chosen = jnp.where(jnp.arange(late)[:, None, None] < image_count, image, text)
    return [jnp.take(chosen, tp ^ k, axis=1) for k in range(tps)]


def body(
    merger_hidden,
    merger_out,
    row_position,
    prompt_embeds,
    norm_gain,
    query_weight,
    key_weight,
    value_weight,
):
    roles, seqs, tps = lax.axis_size("role"), lax.axis_size("seq"), lax.axis_size("tp")
    role, seq, tp = lax.axis_index("role"), lax.axis_index("seq"), lax.axis_index("tp")
    groups = roles * seqs
    rank = role * seqs + seq
    row_count = merger_hidden.shape[0]
    tok_count, columns = prompt_embeds.shape
    strip = merger_out.shape[1]
    part = strip // tps
    late = groups * (2 * row_count // groups)
    early = tok_count - late

    def gather_rows(x):
        mine = jnp.concatenate(gather_xor(x, "seq"), axis=0)
        return jnp.concatenate(gather_xor(mine, "role"), axis=0)

    all_pos = gather_rows(row_position[:, None])[:, 0]
    valid = all_pos >= 0
    owner = jnp.where(valid, all_pos // tok_count, groups)
    lower = (owner[:, None] == owner[None, :]) & (all_pos[None, :] < all_pos[:, None])
    order = jnp.sum(lower.astype(jnp.int32), axis=1)
    device_of = [(role ^ r) * seqs + (seq ^ s) for r in range(roles) for s in range(seqs)]
    targets = jnp.stack(device_of)
    slot_order = jnp.arange(late, dtype=jnp.int32)
    route = (
        (owner[None, None, :] == targets[:, None, None])
        & (order[None, None, :] == slot_order[None, :, None])
    ).astype(BF16)

    tokens = rank * tok_count + jnp.arange(tok_count, dtype=jnp.int32)
    is_image = jnp.any(all_pos[None, :] == tokens[:, None], axis=1)
    earlier = jnp.arange(tok_count)[None, :] < jnp.arange(tok_count)[:, None]
    image_before = jnp.sum((earlier & is_image[None, :]).astype(jnp.int32), axis=1)
    text_before = jnp.arange(tok_count, dtype=jnp.int32) - image_before
    image_count = jnp.sum(is_image.astype(jnp.int32))
    slot = jnp.where(
        is_image,
        early + image_before,
        jnp.where(text_before < early, text_before, text_before + image_count),
    )
    placed = slot[None, :] == jnp.arange(tok_count, dtype=jnp.int32)[:, None]
    early_pick = placed[:early].astype(BF16)
    late_pick = (placed[early:] & ~is_image[None, :]).astype(BF16)
    slot_pos = jnp.sum(jnp.where(placed, tokens[None, :], 0), axis=1)

    early_own = dot(early_pick, prompt_embeds).astype(BF16)
    early_in = jnp.stack(gather_xor(early_own, "tp")[1:])
    gains = jnp.stack(gather_xor(norm_gain[None, :], "tp")).astype(F32)

    hidden = gather_rows(merger_hidden)
    partial_value = dot(hidden, merger_out)
    summed = lax.dynamic_slice_in_dim(partial_value, tp * part, part, axis=1)
    narrow = partial_value.astype(BF16)
    for k in range(1, tps):
        piece = lax.dynamic_slice_in_dim(narrow, (tp ^ k) * part, part, axis=1)
        summed = summed + swap(piece, "tp", k).astype(F32)
    embeds = summed.astype(BF16)

    routed = dot(route.reshape(groups * late, -1), embeds).astype(BF16)
    routed = routed.reshape(roles, seqs, late, part)
    by_role = [routed[0]] + [swap(routed[r], "role", r) for r in range(1, roles)]
    by_role = jnp.stack(by_role, axis=1)
    arrived = [by_role[0]] + [swap(by_role[s], "seq", s) for s in range(1, seqs)]
    image_rows = jnp.concatenate(
        [arrived[s][r] for r in range(roles) for s in range(seqs)], axis=1
    )
    late_own = image_rows + dot(late_pick, prompt_embeds).astype(BF16)
    late_pieces = gather_xor(late_own, "tp")
    if part % 128:
        late_pieces = natural_pieces(late_pieces, part, image_count)
    late_own, late_in = late_pieces[0], jnp.stack(late_pieces[1:])

    half = HEAD_DIM // 2
    frequency = 1000000.0 ** (-jnp.arange(half, dtype=F32) / half)
    angles = slot_pos.astype(F32)[:, None] * frequency[None, :]
    cosine = jnp.concatenate([jnp.cos(angles)] * 2, axis=1)
    sine = jnp.concatenate([-jnp.sin(angles), jnp.sin(angles)], axis=1)

    info = jnp.stack([tp, image_count] + device_of).astype(jnp.int32)
    queries, keys_values, late_rows = project(
        info, early_own, early_in, late_own, late_in, gains, cosine, sine,
        query_weight, key_weight, value_weight, groups,
    )

    local_kv = key_weight.shape[1] // HEAD_DIM
    place_image = (placed[early:] & is_image[None, :]).astype(BF16)
    stream = jnp.where(
        is_image[:, None],
        lax.dot_general(
            place_image, late_rows, (((0,), (0,)), ((), ())), preferred_element_type=F32
        ).astype(BF16),
        prompt_embeds,
    )

    heads_kv = keys_values.shape[1] // 2
    interleaved = jnp.concatenate(
        [
            keys_values[:, side * heads_kv + h * HEAD_DIM : side * heads_kv + (h + 1) * HEAD_DIM]
            for h in range(local_kv)
            for side in range(2)
        ],
        axis=1,
    )
    same_role = gather_xor(interleaved, "seq")
    kvs = list(same_role)
    stacked = jnp.stack(same_role)
    for r in range(1, roles):
        other = swap(stacked, "role", r, lambda a, b: a < b)
        kvs += [other[s] for s in range(seqs)]
    blocks = jnp.stack(device_of).astype(jnp.int32)
    context = attend(
        blocks, queries, kvs, slot_pos[:, None], slot_pos[None, :],
        placed.T.astype(BF16), local_kv,
    )
    return (stream, context)


def solution(mesh):
    in_specs = (
        P(("role", "seq"), "tp"),
        P("tp", ("role", "seq")),
        P(("role", "seq")),
        P(("role", "seq"), "tp"),
        P("tp"),
        P(None, "tp"),
        P(None, "tp"),
        P(None, "tp"),
    )
    out_specs = (P(("role", "seq"), "tp"), P(("role", "seq"), "tp"))
    return jax.shard_map(body, mesh=mesh, in_specs=in_specs, out_specs=out_specs, check_vma=False)
```
